256 devices in a mesh: frame: 32 (over x, z), row: 8 (over y, core).
Axes of the slice: x: 4, y: 4, z: 8, core: 2. Of those that a mesh axis runs over, the one named last changes fastest.
Arguments:
- frames_in: bfloat16 [32, 128, 64, 1152], P('frame', 'row'), may hold values from -6 to 6
- spatial_qkv: bfloat16 [1152, 1728], replicated
- spatial_out: bfloat16 [576, 1152], replicated, may hold values from -0.8984375 to 0.8984375
- temporal_qkv: bfloat16 [1152, 1728], replicated
- temporal_out: bfloat16 [576, 1152], replicated, may hold values from -0.8984375 to 0.8984375
- key_tiles: int32 [32, 128, 9], P('frame', 'row'), may hold values from 0 to 127, as said below
- tile_counts: int32 [32, 128], P('frame', 'row'), may hold values from 1 to 9, as said below
Outputs:
- frames_out: bfloat16 [32, 128, 64, 1152], P('frame', 'row')
The draws below stay inside these ranges and needn't reach their ends.
Inputs may be any that keep to these rules, and one draw needn't show every extreme that they name: `key_tiles`: for query tile t, whose tile row is t // 4 and tile column t % 4, the first tile_counts entries name distinct tiles whose tile row and tile column each differ from t's by at most one; later entries equal t. `tile_counts`: at most the number of tiles within one tile row and one tile column of the query tile.
All inputs are finite; a program needn't handle non-finite values.
Results may differ from the reference program's by a relative error of at most 0.019.
Values may be sent and summed in bfloat16 or wider, within the bound.
A program may use at most 128 MiB of HBM per device.

```python
import jax
import jax.numpy as jnp
from jax import lax

D = 1152
HEADS = 8
HD = 72
TH = 4
TW = 16
KMAX = 9
W = 64
FRAMES = 32
HEIGHT = 128


def qkv_weight(key):
    inner_dim = HEADS * HD
    key_base = jax.random.fold_in(key, 0)
    base_mat = jax.random.normal(key_base, (D, 3 * inner_dim), jnp.float32) * D ** (-0.5)
    return base_mat


def draw_spatial_qkv(key, part):
    return qkv_weight(jax.random.fold_in(key, 11)).astype(jnp.bfloat16)


def draw_temporal_qkv(key, part):
    return qkv_weight(jax.random.fold_in(key, 23)).astype(jnp.bfloat16)


def tile_lists(key):
    key = jax.random.fold_in(key, 7)
    tile_rows = HEIGHT // TH
    tile_cols = W // TW
    tile_ids = jnp.arange(tile_rows * tile_cols, dtype=jnp.int32)
    tile_row = tile_ids // tile_cols
    tile_col = tile_ids % tile_cols
    offsets = jnp.arange(9, dtype=jnp.int32)
    near_row = tile_row[:, None] + (offsets // 3 - 1)[None, :]
    near_col = tile_col[:, None] + (offsets % 3 - 1)[None, :]
    valid = (near_row >= 0) & (near_row < tile_rows) & (near_col >= 0) & (near_col < tile_cols)
    neighbours = jnp.clip(near_row, 0, tile_rows - 1) * tile_cols + jnp.clip(near_col, 0, tile_cols - 1)
    key_order, key_band, key_light = jax.random.split(key, 3)
    ranks = jax.random.randint(key_order, (FRAMES, tile_rows * tile_cols, 9), 0, 1000) * 9 + offsets
    order_key = jnp.where(valid[None], 0, 100000) + ranks
    order = jnp.argsort(order_key, axis=-1)
    lists = jnp.take_along_axis(jnp.broadcast_to(neighbours[None], order.shape), order, axis=-1)
    valid_num = jnp.sum(valid.astype(jnp.int32), axis=-1)
    busy_row = jax.random.randint(key_band, (FRAMES, 1), 0, tile_rows)
    busy_mask = jnp.abs(tile_row[None, :] - busy_row) <= max(tile_rows // 8, 1)
    light_count = jax.random.randint(key_light, (FRAMES, tile_rows * tile_cols), 1, 4)
    counts = jnp.where(busy_mask, valid_num[None], jnp.minimum(light_count, valid_num[None]))
    counts = counts.at[:, tile_cols + 1].set(9)
    lists = jnp.where(offsets[None, None, :] < counts[:, :, None], lists, tile_ids[None, :, None])
    return (lists.astype(jnp.int32), counts.astype(jnp.int32))


def draw_key_tiles(key, part):
    return tile_lists(key)[0]


def draw_tile_counts(key, part):
    return tile_lists(key)[1]


def block_scale(stream_key, extent, cuts, smallest, high):
    level = 1.0
    for axis_at, blocks in cuts:
        steps = jax.random.uniform(jax.random.fold_in(jax.random.fold_in(stream_key, 6), axis_at), (blocks,), jnp.float32, smallest / len(cuts), high / len(cuts))
        level = level * jnp.repeat(jnp.exp(steps), extent[axis_at] // blocks).reshape((-1,) + (1,) * (len(extent) - 1 - axis_at))
    return level


def noise(rng, dims, scale, bound, cuts=(), kind=jnp.bfloat16):
    gain = block_scale(rng, dims, cuts, -0.22, 0.18) if cuts else 1.0
    values = jax.random.normal(rng, dims, jnp.float32) * scale * gain
    return jnp.minimum(jnp.maximum(values, -bound), bound).astype(kind)


def setup_inputs(seed: int = 0) -> dict:
    key_of = jax.random.split(jax.random.key(seed), 8)
    frames_in = noise(key_of[0], (FRAMES, HEIGHT, W, D), 1.0, 6.0, ((0, 32), (1, 8)))
    spatial_qkv = draw_spatial_qkv(jax.random.fold_in(key_of[7], 71), 0)
    spatial_out = noise(key_of[2], (HEADS * HD, D), 0.15, 0.8984375)
    temporal_qkv = draw_temporal_qkv(jax.random.fold_in(key_of[7], 71), 0)
    temporal_out = noise(key_of[4], (HEADS * HD, D), 0.15, 0.8984375)
    key_tiles = draw_key_tiles(jax.random.fold_in(key_of[7], 71), 0)
    tile_counts = draw_tile_counts(jax.random.fold_in(key_of[7], 71), 0)
    return {"frames_in": frames_in, "spatial_qkv": spatial_qkv, "spatial_out": spatial_out, "temporal_qkv": temporal_qkv, "temporal_out": temporal_out, "key_tiles": key_tiles, "tile_counts": tile_counts}


NORM_EPS = 1e-06

def layer_norm(values):
    values = values.astype(jnp.float32)
    centred = values - lax.optimization_barrier(jnp.mean(values, axis=-1, keepdims=True))
    spread = lax.optimization_barrier(jnp.mean(centred * centred, axis=-1, keepdims=True))
    return (centred * lax.rsqrt(spread + NORM_EPS)).astype(jnp.bfloat16)

def softmax_rows(scores):
    top = lax.optimization_barrier(jnp.max(scores, axis=-1, keepdims=True))
    expo = jnp.exp(scores - top)
    return (expo / lax.optimization_barrier(jnp.sum(expo, axis=-1, keepdims=True))).astype(jnp.bfloat16)

def to_tiles(array):
    row_num, col_num, chan_num = array.shape
    shaped = array.reshape(row_num // TH, TH, col_num // TW, TW, chan_num)
    return shaped.transpose(0, 2, 1, 3, 4).reshape(-1, TH * TW, chan_num)

def from_tiles(array, tile_rows, tile_cols):
    chan_num = array.shape[-1]
    shaped = array.reshape(tile_rows, tile_cols, TH, TW, chan_num)
    return shaped.transpose(0, 2, 1, 3, 4).reshape(tile_rows * TH, tile_cols * TW, chan_num)

def tile_attention(queries, key_vecs, val_vecs, counts):
    scores = jnp.einsum('nqhd,nkhd->nhqk', queries.astype(jnp.float32), key_vecs.astype(jnp.float32)) * HD ** (-0.5)
    slot_ids = jnp.arange(key_vecs.shape[1], dtype=jnp.int32) // queries.shape[1]
    live = slot_ids[None, :] < counts[:, None]
    scores = jnp.where(live[:, None, None, :], scores, -1e+30)
    weights = softmax_rows(scores)
    result = jnp.einsum('nhqk,nkhd->nqhd', weights.astype(jnp.float32), val_vecs.astype(jnp.float32))
    return result.astype(jnp.bfloat16)

def temporal_attention(pieces):
    frame_num, pos_num = (pieces.shape[0], pieces.shape[1])
    queries = pieces[:, :, 0].astype(jnp.float32)
    key_vecs = pieces[:, :, 1].astype(jnp.float32)
    val_vecs = pieces[:, :, 2].astype(jnp.float32)
    scores = jnp.einsum('fphd,gphd->phfg', queries, key_vecs) * HD ** (-0.5)
    weights = softmax_rows(scores)
    result = jnp.einsum('phfg,gphd->fphd', weights.astype(jnp.float32), val_vecs)
    return result.astype(jnp.bfloat16).reshape(frame_num, pos_num, HEADS * HD)

def reference(frames_in, spatial_qkv, spatial_out, temporal_qkv, temporal_out, key_tiles, tile_counts):
    inner_dim = HEADS * HD
    height = frames_in.shape[1]
    columns = frames_in.shape[2]
    tile_len = TH * TW

    def spatial_frame(packed):
        frame_in, targets, counts = packed
        normed = layer_norm(frame_in)
        projected = jnp.dot(normed.reshape(height * columns, -1), spatial_qkv, preferred_element_type=jnp.float32)
        projected = projected.astype(jnp.bfloat16).reshape(height, columns, 3 * inner_dim)
        tile_set = to_tiles(projected)
        tile_num = tile_set.shape[0]
        pieces = tile_set.reshape(tile_num, tile_len, 3, HEADS, HD)
        kv_tiles = pieces[:, :, 1:]
        chosen = kv_tiles[targets].reshape(tile_num, KMAX * tile_len, 2, HEADS, HD)
        attended = tile_attention(pieces[:, :, 0], chosen[:, :, 0], chosen[:, :, 1], counts)
        merged = from_tiles(attended.reshape(tile_num, tile_len, inner_dim), height // TH, columns // TW)
        branch = jnp.dot(merged.reshape(-1, inner_dim), spatial_out, preferred_element_type=jnp.float32)
        return (frame_in.astype(jnp.float32) + branch.reshape(height, columns, -1)).astype(jnp.bfloat16)
    mixed_one = lax.map(spatial_frame, (frames_in, key_tiles, tile_counts))
    frame_num = mixed_one.shape[0]
    normed_two = layer_norm(mixed_one)

    def temporal_row(row_slab):
        projected = jnp.dot(row_slab.reshape(-1, row_slab.shape[-1]), temporal_qkv, preferred_element_type=jnp.float32)
        projected = projected.astype(jnp.bfloat16).reshape(frame_num, columns, 3, HEADS, HD)
        return temporal_attention(projected)
    attended = lax.map(temporal_row, jnp.transpose(normed_two, (1, 0, 2, 3)))
    attended = jnp.transpose(attended, (1, 0, 2, 3))
    branch = jnp.dot(attended.reshape(-1, inner_dim), temporal_out, preferred_element_type=jnp.float32)
    return (mixed_one.astype(jnp.float32) + branch.reshape(mixed_one.shape)).astype(jnp.bfloat16)
```

```python
import functools
import math

import jax
import jax.numpy as jnp
from jax import lax
from jax.experimental import pallas as pl
from jax.experimental.pallas import tpu as pltpu
from jax.sharding import PartitionSpec as P

HEADS = 8
HD = 72
TH = 4
TW = 16
INNER = HEADS * HD
PADDED = 640
EPS = 1e-06
NEG = -1e30
SCALE = HD ** (-0.5) * math.log2(math.e)
MESH = pl.DeviceIdType.MESH
F32 = jnp.float32
BF16 = jnp.bfloat16
NT = (((1,), (1,)), ((), ()))


def window(head):
    first, last = head * HD, (head + 1) * HD
    low = first // 128 * 128
    high = -(-last // 128) * 128
    return low, high, first - low, last - low


def layer_norm(values):
    centred = values - jnp.mean(values, axis=-1, keepdims=True)
    spread = jnp.mean(centred * centred, axis=-1, keepdims=True)
    return (centred * lax.rsqrt(spread + EPS)).astype(BF16)


def attend(load_q, load_k, load_v, keep, fill):
    columns = [None] * (PADDED // 128)
    for head in range(HEADS):
        low, high, first, last = window(head)
        query = load_q(low, high)
        lane = lax.broadcasted_iota(jnp.int32, query.shape, 1)
        query = jnp.where((lane >= first) & (lane < last), query, jnp.zeros_like(query))
        scores = lax.dot_general(query, load_k(low, high), NT, preferred_element_type=F32)
        scores = jnp.where(keep, scores, fill)
        top = jnp.max(scores, axis=-1, keepdims=True)
        expo = jnp.exp2(scores - top)
        total = jnp.sum(expo, axis=-1, keepdims=True)
        result = jnp.dot(expo.astype(BF16), load_v(low, high), preferred_element_type=F32)
        result = result * (1.0 / total)
        for part in range((high - low) // 128):
            piece = result[:, part * 128 : (part + 1) * 128]
            at = low // 128 + part
            if columns[at] is None:
                columns[at] = piece
            else:
                spot = lax.broadcasted_iota(jnp.int32, piece.shape, 1) + part * 128
                columns[at] = jnp.where(spot >= first, piece, columns[at])
    spot = lax.broadcasted_iota(jnp.int32, columns[-1].shape, 1)
    columns[-1] = jnp.where(spot < INNER - PADDED + 128, columns[-1], 0.0)
    return jnp.concatenate(columns, axis=1)


def pad_qkv(raw, out):
    depth = raw.shape[0]
    zeros = jnp.zeros((128, PADDED - INNER), BF16)

    def step(i, carry):
        rows = pl.ds(pl.multiple_of(i * 128, 128), 128)
        for part in range(3):
            piece = raw[rows, part * INNER : (part + 1) * INNER]
            out[rows, part * PADDED : (part + 1) * PADDED] = jnp.concatenate([piece, zeros], axis=1)
        return carry

    lax.fori_loop(0, depth // 128, step, 0)


def kernel(
    frames, rows_axis,
    key_tiles, tile_counts, x_hbm, sqkv_hbm, sout_hbm, tqkv_hbm, tout_hbm, out_hbm,
    xbuf, halo, raw_s, raw_t, w_s, w_t, o_s, o_t, qbuf, kbuf, vbuf,
    mixed, landed, heads, back, obuf,
    load_sem, halo_send, halo_recv, go_send, go_recv, back_send, back_recv, store_sem,
):
    frame = lax.axis_index("frame")
    row = lax.axis_index("row")
    above = lax.rem(row + rows_axis - 1, rows_axis)
    below = lax.rem(row + 1, rows_axis)
    feat = x_hbm.shape[-1]
    columns = x_hbm.shape[1]
    slab = TH * columns
    tile_rows = x_hbm.shape[0] // TH
    tile_cols = columns // TW
    tile_len = TH * TW
    group = slab // frames

    barrier = pltpu.get_barrier_semaphore()

    def greet(i, carry):
        pl.semaphore_signal(
            barrier, inc=1, device_id=(lax.rem(frame + i, frames), row), device_id_type=MESH
        )
        return carry

    lax.fori_loop(1, frames, greet, 0)
    for peer in (above, below):
        pl.semaphore_signal(barrier, inc=1, device_id=(frame, peer), device_id_type=MESH)

    loads = [
        pltpu.make_async_copy(src, dst, load_sem.at[i])
        for i, (src, dst) in enumerate(
            (
                (sqkv_hbm, raw_s),
                (x_hbm, xbuf),
                (sout_hbm, o_s.at[pl.ds(0, INNER)]),
                (tqkv_hbm, raw_t),
                (tout_hbm, o_t.at[pl.ds(0, INNER)]),
            )
        )
    ]
    for load in loads:
        load.start()
    pad_rows = jnp.zeros((PADDED - INNER, feat), BF16)
    o_s[INNER:, :] = pad_rows
    o_t[INNER:, :] = pad_rows

    pl.semaphore_wait(barrier, frames + 1)
    send_down = pltpu.make_async_remote_copy(
        x_hbm.at[pl.ds((tile_rows - 1) * TH, TH)], halo.at[0], halo_send.at[0], halo_recv.at[0],
        device_id=(frame, below), device_id_type=MESH,
    )
    send_up = pltpu.make_async_remote_copy(
        x_hbm.at[pl.ds(0, TH)], halo.at[1], halo_send.at[1], halo_recv.at[1],
        device_id=(frame, above), device_id_type=MESH,
    )
    send_down.start()
    send_up.start()

    loads[0].wait()
    pad_qkv(raw_s, w_s)
    loads[1].wait()

    def tiled(ref, first):
        return jnp.concatenate(
            [
                ref[pl.ds(first, TH), c * TW : (c + 1) * TW, :].reshape(tile_len, feat)
                for c in range(tile_cols)
            ],
            axis=0,
        )

    def project(i, carry):
        normed = layer_norm(tiled(xbuf, i * TH).astype(F32))
        result = jnp.dot(normed, w_s[...], preferred_element_type=F32)
        qbuf[i] = (result[:, :PADDED] * SCALE).astype(BF16)
        kbuf[i + 1] = result[:, PADDED : 2 * PADDED].astype(BF16)
        vbuf[i + 1] = result[:, 2 * PADDED :].astype(BF16)
        return carry

    def spatial(i):
        halves = []
        for half in range(2):
            marks = []
            for c in (2 * half, 2 * half + 1):
                tile = i * tile_cols + c
                count = tile_counts[0, tile]
                spot = lax.broadcasted_iota(jnp.int32, (tile_len, 9 * tile_len), 1) // tile_len
                mark = jnp.zeros((tile_len, 9 * tile_len), jnp.int32)
                for slot in range(key_tiles.shape[2]):
                    target = key_tiles[0, tile, slot]
                    down = (target // tile_cols) - (row * tile_rows + i) + 1
                    name = down * 3 + target % tile_cols - half
                    name = jnp.where(slot < count, name, -1)
                    mark = jnp.where(spot == name, 1, mark)
                marks.append(mark)
            keep = jnp.concatenate(marks, axis=0) > 0
            at = half * tile_len

            def load_q(low, high):
                return qbuf[i, 2 * at : 2 * at + 2 * tile_len, low:high]

            def load_keys(ref):
                def load(low, high):
                    return jnp.concatenate(
                        [ref[i + d, at : at + 3 * tile_len, low:high] for d in range(3)], axis=0
                    )

                return load

            halves.append(attend(load_q, load_keys(kbuf), load_keys(vbuf), keep, NEG).astype(BF16))
        attended = jnp.concatenate(halves, axis=0)
        branch = jnp.dot(attended, o_s[...], preferred_element_type=F32)
        result = tiled(xbuf, i * TH).astype(F32) + branch
        mixed[i] = result.reshape(frames, group, feat).astype(BF16)
        landed[i, frame] = mixed[i, frame]

        def send(k, carry):
            peer = lax.rem(frame + k, frames)
            pltpu.make_async_remote_copy(
                mixed.at[i, peer], landed.at[i, frame], go_send.at[i], go_recv.at[i],
                device_id=(peer, row), device_id_type=MESH,
            ).start()
            return carry

        lax.fori_loop(1, frames, send, 0)

    def temporal(i):
        pltpu.make_async_copy(
            landed.at[i, pl.ds(0, frames - 1)], landed.at[i, pl.ds(0, frames - 1)], go_recv.at[i]
        ).wait()
        normed = layer_norm(landed[i].astype(F32).reshape(slab, feat))
        result = jnp.dot(normed, w_t[...], preferred_element_type=F32)
        queries = (result[:, :PADDED] * SCALE).astype(BF16)
        key_vecs = result[:, PADDED : 2 * PADDED].astype(BF16)
        val_vecs = result[:, 2 * PADDED :].astype(BF16)
        mine = lax.broadcasted_iota(jnp.int32, (slab, slab), 0) % group
        theirs = lax.broadcasted_iota(jnp.int32, (slab, slab), 1) % group
        attended = attend(
            lambda low, high: queries[:, low:high],
            lambda low, high: key_vecs[:, low:high],
            lambda low, high: val_vecs[:, low:high],
            mine == theirs,
            -jnp.inf,
        )
        heads[i] = attended.reshape(frames, group, PADDED).astype(BF16)
        back[i, frame] = heads[i, frame]

        def send(k, carry):
            peer = lax.rem(frame + k, frames)
            pltpu.make_async_remote_copy(
                heads.at[i, peer], back.at[i, frame], back_send.at[i], back_recv.at[i],
                device_id=(peer, row), device_id_type=MESH,
            ).start()
            return carry

        lax.fori_loop(1, frames, send, 0)

    def finish(i):
        pltpu.make_async_copy(
            back.at[i, pl.ds(0, frames - 1)], back.at[i, pl.ds(0, frames - 1)], back_recv.at[i]
        ).wait()
        attended = back[i].astype(F32).reshape(slab, PADDED).astype(BF16)
        branch = jnp.dot(attended, o_t[...], preferred_element_type=F32)
        result = (mixed[i].astype(F32).reshape(slab, feat) + branch).astype(BF16)
        for c in range(tile_cols):
            obuf[pl.ds(i * TH, TH), c * TW : (c + 1) * TW, :] = result[
                c * tile_len : (c + 1) * tile_len
            ].reshape(TH, TW, feat)
        pltpu.make_async_copy(
            obuf.at[pl.ds(i * TH, TH)], out_hbm.at[pl.ds(i * TH, TH)], store_sem.at[i]
        ).start()

    lax.fori_loop(0, tile_rows, project, 0)
    loads[2].wait()

    def inner_rows(n, carry):
        spatial(n)
        return carry

    lax.fori_loop(1, tile_rows - 1, inner_rows, 0)

    send_down.wait()
    send_up.wait()

    def project_halo(n, carry):
        normed = layer_norm(tiled(halo.at[n], 0).astype(F32))
        result = jnp.dot(normed, w_s[:, PADDED:], preferred_element_type=F32)
        place = n * (tile_rows + 1)
        kbuf[place] = result[:, :PADDED].astype(BF16)
        vbuf[place] = result[:, PADDED:].astype(BF16)
        return carry

    lax.fori_loop(0, 2, project_halo, 0)

    def outer_rows(n, carry):
        spatial(n * (tile_rows - 1))
        return carry

    lax.fori_loop(0, 2, outer_rows, 0)

    loads[3].wait()
    pad_qkv(raw_t, w_t)
    loads[4].wait()

    def order(n):
        return lax.rem(n + 1, tile_rows)

    def temporal_rows(n, carry):
        temporal(order(n))
        return carry

    lax.fori_loop(0, tile_rows, temporal_rows, 0)

    def finish_rows(n, carry):
        finish(order(n))
        return carry

    lax.fori_loop(0, tile_rows, finish_rows, 0)

    for i in range(tile_rows):
        block = landed.at[i, pl.ds(0, frames - 1)]
        pltpu.make_async_copy(block, block, go_send.at[i]).wait()
        block = back.at[i, pl.ds(0, frames - 1)]
        pltpu.make_async_copy(block, block, back_send.at[i]).wait()
        pltpu.make_async_copy(
            obuf.at[pl.ds(i * TH, TH)], out_hbm.at[pl.ds(i * TH, TH)], store_sem.at[i]
        ).wait()


def body(frames_in, spatial_qkv, spatial_out, temporal_qkv, temporal_out, key_tiles, tile_counts):
    frames = lax.axis_size("frame")
    rows_axis = lax.axis_size("row")
    rows, columns, feat = frames_in.shape[1:]
    slab = TH * columns
    tile_rows = rows // TH
    group = slab // frames
    dma = pltpu.SemaphoreType.DMA
    smem = pl.BlockSpec(memory_space=pltpu.SMEM)
    hbm = pl.BlockSpec(memory_space=pl.ANY)
    result = pl.pallas_call(
        functools.partial(kernel, frames, rows_axis),
        out_shape=jax.ShapeDtypeStruct((rows, columns, feat), BF16),
        in_specs=[smem, smem, hbm, hbm, hbm, hbm, hbm],
        out_specs=hbm,
        scratch_shapes=[
            pltpu.VMEM((rows, columns, feat), BF16),
            pltpu.VMEM((2, TH, columns, feat), BF16),
            pltpu.VMEM((feat, 3 * INNER), BF16),
            pltpu.VMEM((feat, 3 * INNER), BF16),
            pltpu.VMEM((feat, 3 * PADDED), BF16),
            pltpu.VMEM((feat, 3 * PADDED), BF16),
            pltpu.VMEM((PADDED, feat), BF16),
            pltpu.VMEM((PADDED, feat), BF16),
            pltpu.VMEM((tile_rows, slab, PADDED), BF16),
            pltpu.VMEM((tile_rows + 2, slab, PADDED), BF16),
            pltpu.VMEM((tile_rows + 2, slab, PADDED), BF16),
            pltpu.VMEM((tile_rows, frames, group, feat), BF16),
            pltpu.VMEM((tile_rows, frames, group, feat), BF16),
            pltpu.VMEM((tile_rows, frames, group, PADDED), BF16),
            pltpu.VMEM((tile_rows, frames, group, PADDED), BF16),
            pltpu.VMEM((rows, columns, feat), BF16),
            dma((5,)),
            dma((2,)),
            dma((2,)),
            dma((tile_rows,)),
            dma((tile_rows,)),
            dma((tile_rows,)),
            dma((tile_rows,)),
            dma((tile_rows,)),
        ],
        compiler_params=pltpu.CompilerParams(
            collective_id=0, has_side_effects=True, vmem_limit_bytes=67043328
        ),
    )(
        key_tiles, tile_counts, frames_in[0],
        spatial_qkv, spatial_out, temporal_qkv, temporal_out,
    )
    return result[None]


def solution(mesh):
    in_specs = (
        P("frame", "row", None, None),
        P(),
        P(),
        P(),
        P(),
        P("frame", "row", None),
        P("frame", "row"),
    )
    out_specs = P("frame", "row", None, None)
    return jax.shard_map(body, mesh=mesh, in_specs=in_specs, out_specs=out_specs, check_vma=False)
```

```python
import functools
import math

import jax
import jax.numpy as jnp
from jax import lax
from jax.experimental import pallas as pl
from jax.experimental.pallas import tpu as pltpu
from jax.sharding import PartitionSpec as P

HEADS = 8
HD = 72
TH = 4
TW = 16
INNER = HEADS * HD
PADDED = 640
EPS = 1e-06
NEG = -1e30
SCALE = HD ** (-0.5) * math.log2(math.e)
MESH = pl.DeviceIdType.MESH
F32 = jnp.float32
BF16 = jnp.bfloat16
NT = (((1,), (1,)), ((), ()))


def window(head):
    first, last = head * HD, (head + 1) * HD
    low = first // 128 * 128
    high = -(-last // 128) * 128
    return low, high, first - low, last - low


def layer_norm(values):
    centred = values - jnp.mean(values, axis=-1, keepdims=True)
    spread = jnp.mean(centred * centred, axis=-1, keepdims=True)
    return (centred * lax.rsqrt(spread + EPS)).astype(BF16)


def attend(load_q, load_k, load_v, keep, fill):
    columns = [None] * (PADDED // 128)
    for head in range(HEADS):
        low, high, first, last = window(head)
        query = load_q(low, high)
        lane = lax.broadcasted_iota(jnp.int32, query.shape, 1)
        query = jnp.where((lane >= first) & (lane < last), query, jnp.zeros_like(query))
        scores = lax.dot_general(query, load_k(low, high), NT, preferred_element_type=F32)
        scores = jnp.where(keep, scores, fill)
        top = jnp.max(scores, axis=-1, keepdims=True)
        expo = jnp.exp2(scores - top)
        total = jnp.sum(expo, axis=-1, keepdims=True)
        result = jnp.dot(expo.astype(BF16), load_v(low, high), preferred_element_type=F32)
        result = result * (1.0 / total)
        for part in range((high - low) // 128):
            piece = result[:, part * 128 : (part + 1) * 128]
            at = low // 128 + part
            if columns[at] is None:
                columns[at] = piece
            else:
                spot = lax.broadcasted_iota(jnp.int32, piece.shape, 1) + part * 128
                columns[at] = jnp.where(spot >= first, piece, columns[at])
    spot = lax.broadcasted_iota(jnp.int32, columns[-1].shape, 1)
    columns[-1] = jnp.where(spot < INNER - PADDED + 128, columns[-1], 0.0)
    return jnp.concatenate(columns, axis=1)


def kernel(
    frames, rows_axis,
    key_tiles, tile_counts, x_hbm, sqkv_hbm, sout_hbm, tqkv_hbm, tout_hbm, out_hbm,
    xbuf, halo, w_s, w_t, o_s, o_t, qbuf, kbuf, vbuf,
    mixed, landed, heads, rest, tails, back, back_tails, obuf,
    load_sem, halo_send, halo_recv, go_send, go_recv,
    back_send, back_recv, tail_send, tail_recv, store_sem,
):
    frame = lax.axis_index("frame")
    row = lax.axis_index("row")
    above = lax.rem(row + rows_axis - 1, rows_axis)
    below = lax.rem(row + 1, rows_axis)
    feat = x_hbm.shape[-1]
    columns = x_hbm.shape[1]
    slab = TH * columns
    tile_rows = x_hbm.shape[0] // TH
    tile_cols = columns // TW
    tile_len = TH * TW
    group = slab // frames
    half_peers = frames // 2
    parity = lax.rem(frame, 2)
    my_block = parity * half_peers + frame // 2

    barrier = pltpu.get_barrier_semaphore()

    def greet(i, carry):
        pl.semaphore_signal(
            barrier, inc=1, device_id=(lax.rem(frame + i, frames), row), device_id_type=MESH
        )
        return carry

    lax.fori_loop(1, frames, greet, 0)
    for peer in (above, below):
        pl.semaphore_signal(barrier, inc=1, device_id=(frame, peer), device_id_type=MESH)

    def parts(src, dst):
        return [
            (src.at[pl.ds(n * INNER, INNER)], dst.at[pl.ds(n * PADDED, INNER)]) for n in range(3)
        ]

    pairs = [(x_hbm, xbuf)] + parts(sqkv_hbm, w_s) + [(sout_hbm, o_s.at[pl.ds(0, INNER)])]
    pairs += parts(tqkv_hbm, w_t) + [(tout_hbm, o_t.at[pl.ds(0, INNER)])]
    loads = [
        pltpu.make_async_copy(src, dst, load_sem.at[i]) for i, (src, dst) in enumerate(pairs)
    ]
    for load in loads:
        load.start()
    pad_rows = jnp.zeros((PADDED - INNER, feat), BF16)
    for ref in (w_s, w_t):
        for n in range(3):
            ref[n * PADDED + INNER : (n + 1) * PADDED, :] = pad_rows
    o_s[INNER:, :] = pad_rows
    o_t[INNER:, :] = pad_rows

    def tiled(ref, first):
        return jnp.concatenate(
            [
                ref[pl.ds(first, TH), c * TW : (c + 1) * TW, :].reshape(tile_len, feat)
                for c in range(tile_cols)
            ],
            axis=0,
        )

    def project(i, carry):
        normed = layer_norm(tiled(xbuf, i * TH).astype(F32))
        result = lax.dot_general(normed, w_s[...], NT, preferred_element_type=F32)
        qbuf[i] = (result[:, :PADDED] * SCALE).astype(BF16)
        kbuf[i + 1] = result[:, PADDED : 2 * PADDED].astype(BF16)
        vbuf[i + 1] = result[:, 2 * PADDED :].astype(BF16)
        return carry

    def spatial(i):
        rows = tile_rows * row + i
        for half in range(2):
            marks = []
            for c in (2 * half, 2 * half + 1):
                tile = i * tile_cols + c
                count = tile_counts[0, tile]
                spot = lax.broadcasted_iota(jnp.int32, (tile_len, 9 * tile_len), 1) // tile_len
                mark = jnp.zeros((tile_len, 9 * tile_len), jnp.int32)
                for slot in range(key_tiles.shape[0]):
                    target = key_tiles[slot, 0, tile]
                    down = target // tile_cols - rows + 1
                    name = down * 3 + target % tile_cols - half
                    name = jnp.where(slot < count, name, -1)
                    mark = jnp.where(spot == name, 1, mark)
                marks.append(mark)
            keep = jnp.concatenate(marks, axis=0) > 0
            at = half * tile_len
            span = 2 * tile_len

            def load_q(low, high):
                return qbuf[i, 2 * at : 2 * at + span, low:high]

            def load_keys(ref):
                def load(low, high):
                    return jnp.concatenate(
                        [ref[i + d, at : at + 3 * tile_len, low:high] for d in range(3)], axis=0
                    )

                return load

            attended = attend(load_q, load_keys(kbuf), load_keys(vbuf), keep, NEG).astype(BF16)
            branch = jnp.dot(attended, o_s[...], preferred_element_type=F32)
            token = jnp.concatenate(
                [
                    xbuf[pl.ds(i * TH, TH), c * TW : (c + 1) * TW, :].reshape(tile_len, feat)
                    for c in (2 * half, 2 * half + 1)
                ],
                axis=0,
            )
            result = token.astype(F32) + branch
            mixed[i, half * half_peers : (half + 1) * half_peers] = result.reshape(
                half_peers, group, feat
            ).astype(BF16)

            def send(k, carry):
                place = lax.rem(frame // 2 + k, half_peers)
                pltpu.make_async_remote_copy(
                    mixed.at[i, half * half_peers + place], landed.at[i, frame],
                    go_send.at[i], go_recv.at[i],
                    device_id=(2 * place + half, row), device_id_type=MESH,
                ).start()
                return carry

            own = parity if half else 1 - parity
            lax.fori_loop(own, half_peers, send, 0)
        landed[i, frame] = mixed[i, my_block]

    def send_back(src, dst, send_sem, recv_sem):
        def send(k, carry):
            peer = lax.rem(frame + k, frames)
            pltpu.make_async_remote_copy(
                src.at[peer], dst.at[my_block], send_sem, recv_sem,
                device_id=(peer, row), device_id_type=MESH,
            ).start()
            return carry

        dst[my_block] = src[frame]
        lax.fori_loop(1, frames, send, 0)

    def await_all(ref, sem):
        block = ref.at[pl.ds(0, frames - 1)]
        pltpu.make_async_copy(block, block, sem).wait()

    main = PADDED - 128
    left = INNER - main

    def temporal(i, pair, second):
        await_all(landed.at[i], go_recv.at[i])
        normed = layer_norm(landed[i].astype(F32).reshape(slab, feat))
        result = lax.dot_general(normed, w_t[...], NT, preferred_element_type=F32)
        queries = (result[:, :PADDED] * SCALE).astype(BF16)
        key_vecs = result[:, PADDED : 2 * PADDED].astype(BF16)
        val_vecs = result[:, 2 * PADDED :].astype(BF16)
        mine = lax.broadcasted_iota(jnp.int32, (slab, slab), 0) % group
        theirs = lax.broadcasted_iota(jnp.int32, (slab, slab), 1) % group
        attended = attend(
            lambda low, high: queries[:, low:high],
            lambda low, high: key_vecs[:, low:high],
            lambda low, high: val_vecs[:, low:high],
            mine == theirs,
            -jnp.inf,
        )
        heads[i] = attended[:, :main].reshape(frames, group, main).astype(BF16)
        send_back(heads.at[i], back.at[i], back_send.at[i], back_recv.at[i])
        if second:
            lane = lax.broadcasted_iota(jnp.int32, (slab, 128), 1)
            both = jnp.where(lane < left, rest[...], pltpu.roll(attended[:, main:], left, 1))
            tails[pair] = both.reshape(frames, group, 128).astype(BF16)
            send_back(tails.at[pair], back_tails.at[pair], tail_send.at[pair], tail_recv.at[pair])
        else:
            rest[...] = attended[:, main:]

    def finish(i, pair, second):
        await_all(back.at[i], back_recv.at[i])
        if not second:
            await_all(back_tails.at[pair], tail_recv.at[pair])
        tail = back_tails[pair].astype(F32).reshape(slab, 128)
        if second:
            tail = pltpu.roll(tail, left, 1)
        attended = jnp.concatenate([back[i].astype(F32).reshape(slab, main), tail], axis=1)
        branch = jnp.dot(attended.astype(BF16), o_t[...], preferred_element_type=F32)
        result = (mixed[i].astype(F32).reshape(slab, feat) + branch).astype(BF16)
        for c in range(tile_cols):
            obuf[pl.ds(i * TH, TH), c * TW : (c + 1) * TW, :] = result[
                c * tile_len : (c + 1) * tile_len
            ].reshape(TH, TW, feat)
        pltpu.make_async_copy(
            obuf.at[pl.ds(i * TH, TH)], out_hbm.at[pl.ds(i * TH, TH)], store_sem.at[i]
        ).start()

    for load in loads[:4]:
        load.wait()
    lax.fori_loop(0, 2, project, 0)
    loads[4].wait()

    pl.semaphore_wait(barrier, frames + 1)
    send_down = pltpu.make_async_remote_copy(
        x_hbm.at[pl.ds((tile_rows - 1) * TH, TH)], halo.at[0], halo_send.at[0], halo_recv.at[0],
        device_id=(frame, below), device_id_type=MESH,
    )
    send_up = pltpu.make_async_remote_copy(
        x_hbm.at[pl.ds(0, TH)], halo.at[1], halo_send.at[1], halo_recv.at[1],
        device_id=(frame, above), device_id_type=MESH,
    )
    send_down.start()
    send_up.start()

    def inner_rows(n, carry):
        project(n + 1, 0)
        spatial(n)
        return carry

    lax.fori_loop(1, tile_rows - 1, inner_rows, 0)

    send_down.wait()
    send_up.wait()

    def project_halo(n, carry):
        normed = layer_norm(tiled(halo.at[n], 0).astype(F32))
        result = lax.dot_general(normed, w_s[PADDED:, :], NT, preferred_element_type=F32)
        place = n * (tile_rows + 1)
        kbuf[place] = result[:, :PADDED].astype(BF16)
        vbuf[place] = result[:, PADDED:].astype(BF16)
        return carry

    lax.fori_loop(0, 2, project_halo, 0)

    def outer_rows(n, carry):
        spatial(n * (tile_rows - 1))
        return carry

    lax.fori_loop(0, 2, outer_rows, 0)

    for load in loads[5:]:
        load.wait()

    def in_order(step):
        def run(pair, carry):
            for second in range(2):
                step((1 - pair) + second * (1 + (tile_rows - 2) * pair), pair, bool(second))
            return carry

        lax.fori_loop(0, 2, run, 0)

    in_order(temporal)
    in_order(finish)

    for i in range(tile_rows):
        await_all(landed.at[i], go_send.at[i])
        await_all(back.at[i], back_send.at[i])
        pltpu.make_async_copy(
            obuf.at[pl.ds(i * TH, TH)], out_hbm.at[pl.ds(i * TH, TH)], store_sem.at[i]
        ).wait()
    for pair in range(2):
        await_all(back_tails.at[pair], tail_send.at[pair])


def body(frames_in, spatial_qkv, spatial_out, temporal_qkv, temporal_out, key_tiles, tile_counts):
    frames = lax.axis_size("frame")
    rows_axis = lax.axis_size("row")
    rows, columns, feat = frames_in.shape[1:]
    slab = TH * columns
    tile_rows = rows // TH
    group = slab // frames
    dma = pltpu.SemaphoreType.DMA
    smem = pl.BlockSpec(memory_space=pltpu.SMEM)
    hbm = pl.BlockSpec(memory_space=pl.ANY)
    result = pl.pallas_call(
        functools.partial(kernel, frames, rows_axis),
        out_shape=jax.ShapeDtypeStruct((rows, columns, feat), BF16),
        in_specs=[smem, smem, hbm, hbm, hbm, hbm, hbm],
        out_specs=hbm,
        scratch_shapes=[
            pltpu.VMEM((rows, columns, feat), BF16),
            pltpu.VMEM((2, TH, columns, feat), BF16),
            pltpu.VMEM((3 * PADDED, feat), BF16),
            pltpu.VMEM((3 * PADDED, feat), BF16),
            pltpu.VMEM((PADDED, feat), BF16),
            pltpu.VMEM((PADDED, feat), BF16),
            pltpu.VMEM((tile_rows, slab, PADDED), BF16),
            pltpu.VMEM((tile_rows + 2, slab, PADDED), BF16),
            pltpu.VMEM((tile_rows + 2, slab, PADDED), BF16),
            pltpu.VMEM((tile_rows, frames, group, feat), BF16),
            pltpu.VMEM((tile_rows, frames, group, feat), BF16),
            pltpu.VMEM((tile_rows, frames, group, PADDED - 128), BF16),
            pltpu.VMEM((slab, 128), F32),
            pltpu.VMEM((2, frames, group, 128), BF16),
            pltpu.VMEM((tile_rows, frames, group, PADDED - 128), BF16),
            pltpu.VMEM((2, frames, group, 128), BF16),
            pltpu.VMEM((rows, columns, feat), BF16),
            dma((9,)),
            dma((2,)),
            dma((2,)),
            dma((tile_rows,)),
            dma((tile_rows,)),
            dma((tile_rows,)),
            dma((tile_rows,)),
            dma((2,)),
            dma((2,)),
            dma((tile_rows,)),
        ],
        compiler_params=pltpu.CompilerParams(
            collective_id=0, has_side_effects=True, vmem_limit_bytes=67043328
        ),
    )(
        jnp.transpose(key_tiles, (2, 0, 1)), tile_counts, frames_in[0],
        spatial_qkv.T, spatial_out, temporal_qkv.T, temporal_out,
    )
    return result[None]


def solution(mesh):
    in_specs = (
        P("frame", "row", None, None),
        P(),
        P(),
        P(),
        P(),
        P("frame", "row", None),
        P("frame", "row"),
    )
    out_specs = P("frame", "row", None, None)
    return jax.shard_map(body, mesh=mesh, in_specs=in_specs, out_specs=out_specs, check_vma=False)
```

```python
import functools
import math

import jax
import jax.numpy as jnp
from jax import lax
from jax.experimental import pallas as pl
from jax.experimental.pallas import tpu as pltpu
from jax.sharding import PartitionSpec as P

HEADS = 8
HD = 72
TH = 4
TW = 16
INNER = HEADS * HD
PADDED = 640
EPS = 1e-06
NEG = -1e30
SCALE = HD ** (-0.5) * math.log2(math.e)
MESH = pl.DeviceIdType.MESH
F32 = jnp.float32
BF16 = jnp.bfloat16
NT = (((1,), (1,)), ((), ()))


def window(head):
    first, last = head * HD, (head + 1) * HD
    low = first // 128 * 128
    high = -(-last // 128) * 128
    return low, high, first - low, last - low


def layer_norm(values):
    centred = values - jnp.mean(values, axis=-1, keepdims=True)
    spread = jnp.mean(centred * centred, axis=-1, keepdims=True)
    return (centred * lax.rsqrt(spread + EPS)).astype(BF16)


def attend(load_q, load_k, load_v, keep, fill):
    columns = [None] * (PADDED // 128)
    for head in range(HEADS):
        low, high, first, last = window(head)
        query = load_q(low, high)
        lane = lax.broadcasted_iota(jnp.int32, query.shape, 1)
        query = jnp.where((lane >= first) & (lane < last), query, jnp.zeros_like(query))
        scores = lax.dot_general(query, load_k(low, high), NT, preferred_element_type=F32)
        scores = jnp.where(keep, scores, fill)
        top = jnp.max(scores, axis=-1, keepdims=True)
        expo = jnp.exp2(scores - top)
        total = jnp.sum(expo, axis=-1, keepdims=True)
        result = jnp.dot(expo.astype(BF16), load_v(low, high), preferred_element_type=F32)
        result = result * (1.0 / total)
        for part in range((high - low) // 128):
            piece = result[:, part * 128 : (part + 1) * 128]
            at = low // 128 + part
            if columns[at] is None:
                columns[at] = piece
            else:
                spot = lax.broadcasted_iota(jnp.int32, piece.shape, 1) + part * 128
                columns[at] = jnp.where(spot >= first, piece, columns[at])
    spot = lax.broadcasted_iota(jnp.int32, columns[-1].shape, 1)
    columns[-1] = jnp.where(spot < INNER - PADDED + 128, columns[-1], 0.0)
    return jnp.concatenate(columns, axis=1)


def kernel(
    frames, rows_axis,
    tiles_hbm, counts_hbm, x_hbm, sqkv_hbm, sout_hbm, tqkv_hbm, tout_hbm, out_hbm,
    key_tiles, tile_counts, xbuf, halo, w_s, w_t, o_s, o_t, qbuf, kbuf, vbuf,
    mixed, landed, heads, rest, tails, back, back_tails, obuf,
    load_sem, x_sem, halo_send, halo_recv, go_send, go_recv,
    back_send, back_recv, tail_send, tail_recv, store_sem,
):
    frame = lax.axis_index("frame")
    row = lax.axis_index("row")
    above = lax.rem(row + rows_axis - 1, rows_axis)
    below = lax.rem(row + 1, rows_axis)
    feat = x_hbm.shape[-1]
    columns = x_hbm.shape[1]
    slab = TH * columns
    tile_rows = x_hbm.shape[0] // TH
    tile_cols = columns // TW
    tile_len = TH * TW
    group = slab // frames
    half_peers = frames // 2
    parity = lax.rem(frame, 2)
    my_block = parity * half_peers + frame // 2

    barrier = pltpu.get_barrier_semaphore()

    def greet(i, carry):
        pl.semaphore_signal(
            barrier, inc=1, device_id=(lax.rem(frame + i, frames), row), device_id_type=MESH
        )
        return carry

    lax.fori_loop(1, frames, greet, 0)
    for peer in (above, below):
        pl.semaphore_signal(barrier, inc=1, device_id=(frame, peer), device_id_type=MESH)

    def parts(src, dst):
        return [
            (src.at[pl.ds(n * INNER, INNER)], dst.at[pl.ds(n * PADDED, INNER)]) for n in range(3)
        ]

    def load_rows(i):
        block = pl.ds(i * TH, TH)
        return pltpu.make_async_copy(x_hbm.at[block], xbuf.at[block], x_sem.at[i])

    pairs = parts(sqkv_hbm, w_s) + [(sout_hbm, o_s.at[pl.ds(0, INNER)])]
    pairs += [(tiles_hbm, key_tiles), (counts_hbm, tile_counts)]
    pairs += parts(tqkv_hbm, w_t) + [(tout_hbm, o_t.at[pl.ds(0, INNER)])]
    loads = [
        pltpu.make_async_copy(src, dst, load_sem.at[i]) for i, (src, dst) in enumerate(pairs)
    ]
    load_rows(0).start()
    for load in loads[:3]:
        load.start()
    for i in range(1, tile_rows):
        load_rows(i).start()
    for load in loads[3:]:
        load.start()
    pad_rows = jnp.zeros((PADDED - INNER, feat), BF16)
    for ref in (w_s, w_t):
        for n in range(3):
            ref[n * PADDED + INNER : (n + 1) * PADDED, :] = pad_rows
    o_s[INNER:, :] = pad_rows
    o_t[INNER:, :] = pad_rows

    def tiled(ref, first):
        return jnp.concatenate(
            [
                ref[pl.ds(first, TH), c * TW : (c + 1) * TW, :].reshape(tile_len, feat)
                for c in range(tile_cols)
            ],
            axis=0,
        )

    def project_queries(i):
        normed = layer_norm(tiled(xbuf, i * TH).astype(F32))
        result = lax.dot_general(normed, w_s[:PADDED, :], NT, preferred_element_type=F32)
        qbuf[i] = (result * SCALE).astype(BF16)

    def project_keys(ref, first, place):
        normed = layer_norm(tiled(ref, first).astype(F32))
        result = lax.dot_general(normed, w_s[PADDED:, :], NT, preferred_element_type=F32)
        kbuf[place] = result[:, :PADDED].astype(BF16)
        vbuf[place] = result[:, PADDED:].astype(BF16)

    def spatial(i, before_send):
        rows = tile_rows * row + i
        for half in range(2):
            marks = []
            for c in (2 * half, 2 * half + 1):
                tile = i * tile_cols + c
                count = tile_counts[0, tile]
                spot = lax.broadcasted_iota(jnp.int32, (tile_len, 9 * tile_len), 1) // tile_len
                mark = jnp.zeros((tile_len, 9 * tile_len), jnp.int32)
                for slot in range(key_tiles.shape[0]):
                    target = key_tiles[slot, 0, tile]
                    down = target // tile_cols - rows + 1
                    name = down * 3 + target % tile_cols - half
                    name = jnp.where(slot < count, name, -1)
                    mark = jnp.where(spot == name, 1, mark)
                marks.append(mark)
            keep = jnp.concatenate(marks, axis=0) > 0
            at = half * tile_len
            span = 2 * tile_len

            def load_q(low, high):
                return qbuf[i, 2 * at : 2 * at + span, low:high]

            def load_keys(ref):
                def load(low, high):
                    return jnp.concatenate(
                        [ref[i + d, at : at + 3 * tile_len, low:high] for d in range(3)], axis=0
                    )

                return load

            attended = attend(load_q, load_keys(kbuf), load_keys(vbuf), keep, NEG).astype(BF16)
            branch = jnp.dot(attended, o_s[...], preferred_element_type=F32)
            token = jnp.concatenate(
                [
                    xbuf[pl.ds(i * TH, TH), c * TW : (c + 1) * TW, :].reshape(tile_len, feat)
                    for c in (2 * half, 2 * half + 1)
                ],
                axis=0,
            )
            result = token.astype(F32) + branch
            mixed[i, half * half_peers : (half + 1) * half_peers] = result.reshape(
                half_peers, group, feat
            ).astype(BF16)

            if half == 0:
                before_send()

            def send(k, carry):
                place = lax.rem(frame // 2 + k, half_peers)
                pltpu.make_async_remote_copy(
                    mixed.at[i, half * half_peers + place], landed.at[i, frame],
                    go_send.at[i], go_recv.at[i],
                    device_id=(2 * place + half, row), device_id_type=MESH,
                ).start()
                return carry

            own = parity if half else 1 - parity
            lax.fori_loop(own, half_peers, send, 0)
        landed[i, frame] = mixed[i, my_block]

    def send_back(src, dst, send_sem, recv_sem):
        def send(k, carry):
            peer = lax.rem(frame + k, frames)
            pltpu.make_async_remote_copy(
                src.at[peer], dst.at[my_block], send_sem, recv_sem,
                device_id=(peer, row), device_id_type=MESH,
            ).start()
            return carry

        dst[my_block] = src[frame]
        lax.fori_loop(1, frames, send, 0)

    def await_all(ref, sem):
        block = ref.at[pl.ds(0, frames - 1)]
        pltpu.make_async_copy(block, block, sem).wait()

    main = PADDED - 128
    left = INNER - main

    def temporal(i, pair, second):
        await_all(landed.at[i], go_recv.at[i])
        normed = layer_norm(landed[i].astype(F32).reshape(slab, feat))
        result = lax.dot_general(normed, w_t[...], NT, preferred_element_type=F32)
        queries = (result[:, :PADDED] * SCALE).astype(BF16)
        key_vecs = result[:, PADDED : 2 * PADDED].astype(BF16)
        val_vecs = result[:, 2 * PADDED :].astype(BF16)
        mine = lax.broadcasted_iota(jnp.int32, (slab, slab), 0) % group
        theirs = lax.broadcasted_iota(jnp.int32, (slab, slab), 1) % group
        attended = attend(
            lambda low, high: queries[:, low:high],
            lambda low, high: key_vecs[:, low:high],
            lambda low, high: val_vecs[:, low:high],
            mine == theirs,
            -jnp.inf,
        )
        heads[i] = attended[:, :main].reshape(frames, group, main).astype(BF16)
        if second:
            lane = lax.broadcasted_iota(jnp.int32, (slab, 128), 1)
            both = jnp.where(lane < left, rest[...], pltpu.roll(attended[:, main:], left, 1))
            tails[pair] = both.reshape(frames, group, 128).astype(BF16)
        else:
            rest[...] = attended[:, main:]

    def send_heads(i):
        send_back(heads.at[i], back.at[i], back_send.at[i], back_recv.at[i])

    def send_tails(pair):
        send_back(tails.at[pair], back_tails.at[pair], tail_send.at[pair], tail_recv.at[pair])

    def finish(i, pair, second):
        await_all(back.at[i], back_recv.at[i])
        if not second:
            await_all(back_tails.at[pair], tail_recv.at[pair])
        tail = back_tails[pair].astype(F32).reshape(slab, 128)
        if second:
            tail = pltpu.roll(tail, left, 1)
        attended = jnp.concatenate([back[i].astype(F32).reshape(slab, main), tail], axis=1)
        branch = jnp.dot(attended.astype(BF16), o_t[...], preferred_element_type=F32)
        result = (mixed[i].astype(F32).reshape(slab, feat) + branch).astype(BF16)
        for c in range(tile_cols):
            obuf[pl.ds(i * TH, TH), c * TW : (c + 1) * TW, :] = result[
                c * tile_len : (c + 1) * tile_len
            ].reshape(TH, TW, feat)
        pltpu.make_async_copy(
            obuf.at[pl.ds(i * TH, TH)], out_hbm.at[pl.ds(i * TH, TH)], store_sem.at[i]
        ).start()

    load_rows(0).wait()
    for load in loads[:3]:
        load.wait()
    last = tile_rows - 1

    def first_keys(i, carry):
        @pl.when(i > 0)
        def _():
            load_rows(i).wait()

        project_keys(xbuf, i * TH, i + 1)
        return carry

    lax.fori_loop(0, last, first_keys, 0)
    project_queries(1)
    for load in loads[3:6]:
        load.wait()

    send_down = pltpu.make_async_remote_copy(
        x_hbm.at[pl.ds(last * TH, TH)], halo.at[0], halo_send.at[0], halo_recv.at[0],
        device_id=(frame, below), device_id_type=MESH,
    )
    send_up = pltpu.make_async_remote_copy(
        x_hbm.at[pl.ds(0, TH)], halo.at[1], halo_send.at[1], halo_recv.at[1],
        device_id=(frame, above), device_id_type=MESH,
    )

    def meet():
        pl.semaphore_wait(barrier, frames + 1)
        send_down.start()
        send_up.start()

    spatial(1, meet)
    load_rows(last).wait()
    project_keys(xbuf, last * TH, tile_rows)

    def other_rows(n, carry):
        @pl.when(n == 1)
        def _():
            send_down.wait()
            send_up.wait()

            def halo_keys(k, carry):
                project_keys(halo.at[k], 0, k * (tile_rows + 1))
                return carry

            lax.fori_loop(0, 2, halo_keys, 0)

        i = jnp.where(n == 0, 2, (n - 1) * last)
        project_queries(i)
        spatial(i, lambda: None)
        return carry

    lax.fori_loop(0, last, other_rows, 0)

    for load in loads[6:]:
        load.wait()

    def place_of(pair, second):
        return (1 - pair) + second * (1 + (tile_rows - 2) * pair)

    def temporal_pair(pair, carry):
        temporal(place_of(pair, 0), pair, False)

        @pl.when(pair == 1)
        def _():
            for i in range(tile_rows):
                await_all(landed.at[i], go_send.at[i])
            send_heads(1)
            send_heads(2)
            send_tails(0)
            send_heads(0)

        temporal(place_of(pair, 1), pair, True)
        return carry

    lax.fori_loop(0, 2, temporal_pair, 0)
    send_heads(last)
    send_tails(1)

    def finish_pair(pair, carry):
        for second in range(2):
            finish(place_of(pair, second), pair, bool(second))
        return carry

    lax.fori_loop(0, 2, finish_pair, 0)

    for i in range(tile_rows):
        await_all(back.at[i], back_send.at[i])
        pltpu.make_async_copy(
            obuf.at[pl.ds(i * TH, TH)], out_hbm.at[pl.ds(i * TH, TH)], store_sem.at[i]
        ).wait()
    for pair in range(2):
        await_all(back_tails.at[pair], tail_send.at[pair])


def body(frames_in, spatial_qkv, spatial_out, temporal_qkv, temporal_out, key_tiles, tile_counts):
    frames = lax.axis_size("frame")
    rows_axis = lax.axis_size("row")
    rows, columns, feat = frames_in.shape[1:]
    slab = TH * columns
    tile_rows = rows // TH
    group = slab // frames
    dma = pltpu.SemaphoreType.DMA
    hbm = pl.BlockSpec(memory_space=pltpu.HBM)
    result = pl.pallas_call(
        functools.partial(kernel, frames, rows_axis),
        out_shape=jax.ShapeDtypeStruct((rows, columns, feat), BF16),
        in_specs=[hbm] * 7,
        out_specs=pl.BlockSpec(memory_space=pl.ANY),
        scratch_shapes=[
            pltpu.SMEM(key_tiles.shape[2:] + (1, key_tiles.shape[1]), jnp.int32),
            pltpu.SMEM(tile_counts.shape, jnp.int32),
            pltpu.VMEM((rows, columns, feat), BF16),
            pltpu.VMEM((2, TH, columns, feat), BF16),
            pltpu.VMEM((3 * PADDED, feat), BF16),
            pltpu.VMEM((3 * PADDED, feat), BF16),
            pltpu.VMEM((PADDED, feat), BF16),
            pltpu.VMEM((PADDED, feat), BF16),
            pltpu.VMEM((tile_rows, slab, PADDED), BF16),
            pltpu.VMEM((tile_rows + 2, slab, PADDED), BF16),
            pltpu.VMEM((tile_rows + 2, slab, PADDED), BF16),
            pltpu.VMEM((tile_rows, frames, group, feat), BF16),
            pltpu.VMEM((tile_rows, frames, group, feat), BF16),
            pltpu.VMEM((tile_rows, frames, group, PADDED - 128), BF16),
            pltpu.VMEM((slab, 128), F32),
            pltpu.VMEM((2, frames, group, 128), BF16),
            pltpu.VMEM((tile_rows, frames, group, PADDED - 128), BF16),
            pltpu.VMEM((2, frames, group, 128), BF16),
            pltpu.VMEM((rows, columns, feat), BF16),
            dma((10,)),
            dma((tile_rows,)),
            dma((2,)),
            dma((2,)),
            dma((tile_rows,)),
            dma((tile_rows,)),
            dma((tile_rows,)),
            dma((tile_rows,)),
            dma((2,)),
            dma((2,)),
            dma((tile_rows,)),
        ],
        compiler_params=pltpu.CompilerParams(
            collective_id=0, has_side_effects=True, vmem_limit_bytes=44 * 2**20
        ),
    )(
        *(
            pltpu.with_memory_space_constraint(array, pltpu.HBM)
            for array in (
                jnp.transpose(key_tiles, (2, 0, 1)), tile_counts, frames_in[0],
                spatial_qkv.T, spatial_out, temporal_qkv.T, temporal_out,
            )
        )
    )
    return result[None]


def solution(mesh):
    in_specs = (
        P("frame", "row", None, None),
        P(),
        P(),
        P(),
        P(),
        P("frame", "row", None),
        P("frame", "row"),
    )
    out_specs = P("frame", "row", None, None)
    return jax.shard_map(body, mesh=mesh, in_specs=in_specs, out_specs=out_specs, check_vma=False)
```

```python
import functools
import math

import jax
import jax.numpy as jnp
from jax import lax
from jax.experimental import pallas as pl
from jax.experimental.pallas import tpu as pltpu
from jax.sharding import PartitionSpec as P

HEADS = 8
HD = 72
TH = 4
TW = 16
INNER = HEADS * HD
PADDED = 640
EPS = 1e-06
NEG = -1e30
SCALE = HD ** (-0.5) * math.log2(math.e)
MESH = pl.DeviceIdType.MESH
F32 = jnp.float32
BF16 = jnp.bfloat16
NT = (((1,), (1,)), ((), ()))


def window(head):
    first, last = head * HD, (head + 1) * HD
    low = first // 128 * 128
    high = -(-last // 128) * 128
    return low, high, first - low, last - low


def layer_norm(values):
    centred = values - jnp.mean(values, axis=-1, keepdims=True)
    spread = jnp.mean(centred * centred, axis=-1, keepdims=True)
    return (centred * lax.rsqrt(spread + EPS)).astype(BF16)


def attend(load_q, load_k, load_v, keep, fill):
    columns = [None] * (PADDED // 128)
    for head in range(HEADS):
        low, high, first, last = window(head)
        query = load_q(low, high)
        lane = lax.broadcasted_iota(jnp.int32, query.shape, 1)
        query = jnp.where((lane >= first) & (lane < last), query, jnp.zeros_like(query))
        scores = lax.dot_general(query, load_k(low, high), NT, preferred_element_type=F32)
        scores = jnp.where(keep, scores, fill)
        top = jnp.max(scores, axis=-1, keepdims=True)
        expo = jnp.exp2(scores - top)
        total = jnp.sum(expo, axis=-1, keepdims=True)
        result = jnp.dot(expo.astype(BF16), load_v(low, high), preferred_element_type=F32)
        result = result * (1.0 / total)
        for part in range((high - low) // 128):
            piece = result[:, part * 128 : (part + 1) * 128]
            at = low // 128 + part
            if columns[at] is None:
                columns[at] = piece
            else:
                spot = lax.broadcasted_iota(jnp.int32, piece.shape, 1) + part * 128
                columns[at] = jnp.where(spot >= first, piece, columns[at])
    spot = lax.broadcasted_iota(jnp.int32, columns[-1].shape, 1)
    columns[-1] = jnp.where(spot < INNER - PADDED + 128, columns[-1], 0.0)
    return jnp.concatenate(columns, axis=1)


def kernel(
    frames, rows_axis,
    tiles_hbm, counts_hbm, x_hbm, sqkv_hbm, sout_hbm, tqkv_hbm, tout_hbm, out_hbm,
    key_tiles, tile_counts, xbuf, halo, w_s, w_t, o_s, o_t, qbuf, kbuf, vbuf,
    mixed, landed, heads, long_heads, rest, back, long_back, obuf,
    load_sem, x_sem, halo_send, halo_recv, go_send, go_recv,
    back_send, back_recv, long_send, long_recv, store_sem,
):
    frame = lax.axis_index("frame")
    row = lax.axis_index("row")
    above = lax.rem(row + rows_axis - 1, rows_axis)
    below = lax.rem(row + 1, rows_axis)
    feat = x_hbm.shape[-1]
    columns = x_hbm.shape[1]
    slab = TH * columns
    tile_rows = x_hbm.shape[0] // TH
    tile_cols = columns // TW
    tile_len = TH * TW
    group = slab // frames
    half_peers = frames // 2
    parity = lax.rem(frame, 2)
    my_block = parity * half_peers + frame // 2

    barrier = pltpu.get_barrier_semaphore()

    def greet(i, carry):
        pl.semaphore_signal(
            barrier, inc=1, device_id=(lax.rem(frame + i, frames), row), device_id_type=MESH
        )
        return carry

    lax.fori_loop(1, frames, greet, 0)
    for peer in (above, below):
        pl.semaphore_signal(barrier, inc=1, device_id=(frame, peer), device_id_type=MESH)

    def parts(src, dst):
        return [
            (src.at[pl.ds(n * INNER, INNER)], dst.at[pl.ds(n * PADDED, INNER)]) for n in (1, 2, 0)
        ]

    def load_rows(i):
        block = pl.ds(i * TH, TH)
        return pltpu.make_async_copy(x_hbm.at[block], xbuf.at[block], x_sem.at[i])

    pairs = parts(sqkv_hbm, w_s) + [(sout_hbm, o_s.at[pl.ds(0, INNER)])]
    pairs += [(tiles_hbm, key_tiles), (counts_hbm, tile_counts)]
    pairs += parts(tqkv_hbm, w_t) + [(tout_hbm, o_t.at[pl.ds(0, INNER)])]
    loads = [
        pltpu.make_async_copy(src, dst, load_sem.at[i]) for i, (src, dst) in enumerate(pairs)
    ]
    load_rows(0).start()
    for load in loads[:2]:
        load.start()
    for i in range(1, tile_rows - 1):
        load_rows(i).start()
    for load in loads[2:6]:
        load.start()
    load_rows(tile_rows - 1).start()
    for load in loads[6:]:
        load.start()
    pad_rows = jnp.zeros((PADDED - INNER, feat), BF16)
    for ref in (w_s, w_t):
        for n in range(3):
            ref[n * PADDED + INNER : (n + 1) * PADDED, :] = pad_rows
    o_s[INNER:, :] = pad_rows
    o_t[INNER:, :] = pad_rows

    def tiled(ref, first, low=0, high=tile_cols):
        return jnp.concatenate(
            [
                ref[pl.ds(first, TH), c * TW : (c + 1) * TW, :].reshape(tile_len, feat)
                for c in range(low, high)
            ],
            axis=0,
        )

    def project_queries(i, low=0, high=tile_cols):
        normed = layer_norm(tiled(xbuf, i * TH, low, high).astype(F32))
        result = lax.dot_general(normed, w_s[:PADDED, :], NT, preferred_element_type=F32)
        qbuf[i, low * tile_len : high * tile_len] = (result * SCALE).astype(BF16)

    def project_keys(ref, first, place):
        normed = layer_norm(tiled(ref, first).astype(F32))
        result = lax.dot_general(normed, w_s[PADDED:, :], NT, preferred_element_type=F32)
        kbuf[place] = result[:, :PADDED].astype(BF16)
        vbuf[place] = result[:, PADDED:].astype(BF16)

    def spatial(i, before_half, before_send):
        rows = tile_rows * row + i
        for half in range(2):
            before_half(half)
            marks = []
            for c in (2 * half, 2 * half + 1):
                tile = i * tile_cols + c
                count = tile_counts[0, tile]
                spot = lax.broadcasted_iota(jnp.int32, (tile_len, 9 * tile_len), 1) // tile_len
                mark = jnp.zeros((tile_len, 9 * tile_len), jnp.int32)
                for slot in range(key_tiles.shape[0]):
                    target = key_tiles[slot, 0, tile]
                    down = target // tile_cols - rows + 1
                    name = down * 3 + target % tile_cols - half
                    name = jnp.where(slot < count, name, -1)
                    mark = jnp.where(spot == name, 1, mark)
                marks.append(mark)
            keep = jnp.concatenate(marks, axis=0) > 0
            at = half * tile_len
            span = 2 * tile_len

            def load_q(low, high):
                return qbuf[i, 2 * at : 2 * at + span, low:high]

            def load_keys(ref):
                def load(low, high):
                    return jnp.concatenate(
                        [ref[i + d, at : at + 3 * tile_len, low:high] for d in range(3)], axis=0
                    )

                return load

            attended = attend(load_q, load_keys(kbuf), load_keys(vbuf), keep, NEG).astype(BF16)
            branch = jnp.dot(attended, o_s[...], preferred_element_type=F32)
            token = tiled(xbuf, i * TH, 2 * half, 2 * half + 2)
            result = token.astype(F32) + branch
            mixed[i, half * half_peers : (half + 1) * half_peers] = result.reshape(
                half_peers, group, feat
            ).astype(BF16)

            if half == 0:
                before_send()

            def send(k, carry):
                place = lax.rem(frame // 2 + k, half_peers)
                pltpu.make_async_remote_copy(
                    mixed.at[i, half * half_peers + place], landed.at[i, frame],
                    go_send.at[i], go_recv.at[i],
                    device_id=(2 * place + half, row), device_id_type=MESH,
                ).start()
                return carry

            own = parity if half else 1 - parity
            lax.fori_loop(own, half_peers, send, 0)
        landed[i, frame] = mixed[i, my_block]

    def send_back(src, dst, send_sem, recv_sem):
        def send(k, carry):
            peer = lax.rem(frame + k, frames)
            pltpu.make_async_remote_copy(
                src.at[peer], dst.at[my_block], send_sem, recv_sem,
                device_id=(peer, row), device_id_type=MESH,
            ).start()
            return carry

        dst[my_block] = src[frame]
        lax.fori_loop(1, frames, send, 0)

    def await_all(ref, sem):
        block = ref.at[pl.ds(0, frames - 1)]
        pltpu.make_async_copy(block, block, sem).wait()

    main = PADDED - 128
    left = INNER - main

    def temporal(i, pair, second):
        await_all(landed.at[i], go_recv.at[i])
        normed = layer_norm(landed[i].astype(F32).reshape(slab, feat))
        result = lax.dot_general(normed, w_t[...], NT, preferred_element_type=F32)
        queries = (result[:, :PADDED] * SCALE).astype(BF16)
        key_vecs = result[:, PADDED : 2 * PADDED].astype(BF16)
        val_vecs = result[:, 2 * PADDED :].astype(BF16)
        mine = lax.broadcasted_iota(jnp.int32, (slab, slab), 0) % group
        theirs = lax.broadcasted_iota(jnp.int32, (slab, slab), 1) % group
        attended = attend(
            lambda low, high: queries[:, low:high],
            lambda low, high: key_vecs[:, low:high],
            lambda low, high: val_vecs[:, low:high],
            mine == theirs,
            -jnp.inf,
        )
        if second:
            lane = lax.broadcasted_iota(jnp.int32, (slab, 128), 1)
            both = jnp.where(lane < left, rest[...], pltpu.roll(attended[:, main:], left, 1))
            whole = jnp.concatenate([attended[:, :main], both], axis=1)
            long_heads[pair] = whole.reshape(frames, group, PADDED).astype(BF16)
        else:
            heads[pair] = attended[:, :main].reshape(frames, group, main).astype(BF16)
            rest[...] = attended[:, main:]

    def send_first(pair):
        send_back(heads.at[pair], back.at[pair], back_send.at[pair], back_recv.at[pair])

    def send_second(pair):
        send_back(
            long_heads.at[pair], long_back.at[pair], long_send.at[pair], long_recv.at[pair]
        )

    def finish(i, pair, second):
        if second:
            long = long_back[pair].astype(F32).reshape(slab, PADDED)
            part = long[:, :main]
            tail = pltpu.roll(long[:, main:], left, 1)
        else:
            await_all(back.at[pair], back_recv.at[pair])
            await_all(long_back.at[pair], long_recv.at[pair])
            part = back[pair].astype(F32).reshape(slab, main)
            tail = long_back[pair, :, :, main:].astype(F32).reshape(slab, 128)
        attended = jnp.concatenate([part, tail], axis=1)
        branch = jnp.dot(attended.astype(BF16), o_t[...], preferred_element_type=F32)
        result = (mixed[i].astype(F32).reshape(slab, feat) + branch).astype(BF16)
        for c in range(tile_cols):
            obuf[pl.ds(i * TH, TH), c * TW : (c + 1) * TW, :] = result[
                c * tile_len : (c + 1) * tile_len
            ].reshape(TH, TW, feat)
        pltpu.make_async_copy(
            obuf.at[pl.ds(i * TH, TH)], out_hbm.at[pl.ds(i * TH, TH)], store_sem.at[i]
        ).start()

    load_rows(0).wait()
    for load in loads[:2]:
        load.wait()
    last = tile_rows - 1

    def first_keys(i, carry):
        @pl.when(i > 0)
        def _():
            load_rows(i).wait()

        project_keys(xbuf, i * TH, i + 1)
        return carry

    lax.fori_loop(0, last, first_keys, 0)
    for load in loads[2:6]:
        load.wait()

    send_down = pltpu.make_async_remote_copy(
        x_hbm.at[pl.ds(last * TH, TH)], halo.at[0], halo_send.at[0], halo_recv.at[0],
        device_id=(frame, below), device_id_type=MESH,
    )
    send_up = pltpu.make_async_remote_copy(
        x_hbm.at[pl.ds(0, TH)], halo.at[1], halo_send.at[1], halo_recv.at[1],
        device_id=(frame, above), device_id_type=MESH,
    )

    def meet():
        pl.semaphore_wait(barrier, frames + 1)
        send_down.start()
        send_up.start()

    spatial(1, lambda half: project_queries(1, 2 * half, 2 * half + 2), meet)
    load_rows(last).wait()
    project_keys(xbuf, last * TH, tile_rows)

    def other_rows(n, carry):
        @pl.when(n == 1)
        def _():
            send_down.wait()
            send_up.wait()

            def halo_keys(k, carry):
                project_keys(halo.at[k], 0, k * (tile_rows + 1))
                return carry

            lax.fori_loop(0, 2, halo_keys, 0)

        i = jnp.where(n == 0, 2, (n - 1) * last)
        project_queries(i)
        spatial(i, lambda half: None, lambda: None)
        return carry

    lax.fori_loop(0, last, other_rows, 0)

    for load in loads[6:]:
        load.wait()

    def place_of(pair, second):
        return (1 - pair) + second * (1 + (tile_rows - 2) * pair)

    def temporal_pair(pair, carry):
        temporal(place_of(pair, 0), pair, False)

        @pl.when(pair == 1)
        def _():
            for i in range(tile_rows):
                await_all(landed.at[i], go_send.at[i])
            send_first(0)
            send_second(0)
            send_first(1)

        temporal(place_of(pair, 1), pair, True)
        return carry

    lax.fori_loop(0, 2, temporal_pair, 0)
    send_second(1)

    def finish_pair(pair, carry):
        for second in range(2):
            finish(place_of(pair, second), pair, bool(second))
        return carry

    lax.fori_loop(0, 2, finish_pair, 0)

    for pair in range(2):
        await_all(back.at[pair], back_send.at[pair])
        await_all(long_back.at[pair], long_send.at[pair])
    for i in range(tile_rows):
        pltpu.make_async_copy(
            obuf.at[pl.ds(i * TH, TH)], out_hbm.at[pl.ds(i * TH, TH)], store_sem.at[i]
        ).wait()


def body(frames_in, spatial_qkv, spatial_out, temporal_qkv, temporal_out, key_tiles, tile_counts):
    frames = lax.axis_size("frame")
    rows_axis = lax.axis_size("row")
    rows, columns, feat = frames_in.shape[1:]
    slab = TH * columns
    tile_rows = rows // TH
    group = slab // frames
    dma = pltpu.SemaphoreType.DMA
    hbm = pl.BlockSpec(memory_space=pltpu.HBM)
    result = pl.pallas_call(
        functools.partial(kernel, frames, rows_axis),
        out_shape=jax.ShapeDtypeStruct((rows, columns, feat), BF16),
        in_specs=[hbm] * 7,
        out_specs=pl.BlockSpec(memory_space=pl.ANY),
        scratch_shapes=[
            pltpu.SMEM(key_tiles.shape[2:] + (1, key_tiles.shape[1]), jnp.int32),
            pltpu.SMEM(tile_counts.shape, jnp.int32),
            pltpu.VMEM((rows, columns, feat), BF16),
            pltpu.VMEM((2, TH, columns, feat), BF16),
            pltpu.VMEM((3 * PADDED, feat), BF16),
            pltpu.VMEM((3 * PADDED, feat), BF16),
            pltpu.VMEM((PADDED, feat), BF16),
            pltpu.VMEM((PADDED, feat), BF16),
            pltpu.VMEM((tile_rows, slab, PADDED), BF16),
            pltpu.VMEM((tile_rows + 2, slab, PADDED), BF16),
            pltpu.VMEM((tile_rows + 2, slab, PADDED), BF16),
            pltpu.VMEM((tile_rows, frames, group, feat), BF16),
            pltpu.VMEM((tile_rows, frames, group, feat), BF16),
            pltpu.VMEM((2, frames, group, PADDED - 128), BF16),
            pltpu.VMEM((2, frames, group, PADDED), BF16),
            pltpu.VMEM((slab, 128), F32),
            pltpu.VMEM((2, frames, group, PADDED - 128), BF16),
            pltpu.VMEM((2, frames, group, PADDED), BF16),
            pltpu.VMEM((rows, columns, feat), BF16),
            dma((10,)),
            dma((tile_rows,)),
            dma((2,)),
            dma((2,)),
            dma((tile_rows,)),
            dma((tile_rows,)),
            dma((2,)),
            dma((2,)),
            dma((2,)),
            dma((2,)),
            dma((tile_rows,)),
        ],
        compiler_params=pltpu.CompilerParams(
            collective_id=0, has_side_effects=True, vmem_limit_bytes=44 * 2**20
        ),
    )(
        *(
            pltpu.with_memory_space_constraint(array, pltpu.HBM)
            for array in (
                jnp.transpose(key_tiles, (2, 0, 1)), tile_counts, frames_in[0],
                spatial_qkv.T, spatial_out, temporal_qkv.T, temporal_out,
            )
        )
    )
    return result[None]


def solution(mesh):
    in_specs = (
        P("frame", "row", None, None),
        P(),
        P(),
        P(),
        P(),
        P("frame", "row", None),
        P("frame", "row"),
    )
    out_specs = P("frame", "row", None, None)
    return jax.shard_map(body, mesh=mesh, in_specs=in_specs, out_specs=out_specs, check_vma=False)
```

```python
import functools
import math

import jax
import jax.numpy as jnp
from jax import lax
from jax.experimental import pallas as pl
from jax.experimental.pallas import tpu as pltpu
from jax.sharding import PartitionSpec as P

HEADS = 8
HD = 72
TH = 4
TW = 16
INNER = HEADS * HD
PADDED = 640
EPS = 1e-06
NEG = -1e30
SCALE = HD ** (-0.5) * math.log2(math.e)
MESH = pl.DeviceIdType.MESH
F32 = jnp.float32
BF16 = jnp.bfloat16
NT = (((1,), (1,)), ((), ()))


def window(head):
    first, last = head * HD, (head + 1) * HD
    low = first // 128 * 128
    high = -(-last // 128) * 128
    return low, high, first - low, last - low


def layer_norm(values):
    centred = values - jnp.mean(values, axis=-1, keepdims=True)
    spread = jnp.mean(centred * centred, axis=-1, keepdims=True)
    return (centred * lax.rsqrt(spread + EPS)).astype(BF16)


def attend(load_q, load_k, load_v, keep, fill):
    columns = [None] * (PADDED // 128)
    for head in range(HEADS):
        low, high, first, last = window(head)
        query = load_q(low, high)
        lane = lax.broadcasted_iota(jnp.int32, query.shape, 1)
        query = jnp.where((lane >= first) & (lane < last), query, jnp.zeros_like(query))
        scores = lax.dot_general(query, load_k(low, high), NT, preferred_element_type=F32)
        scores = jnp.where(keep, scores, fill)
        top = jnp.max(scores, axis=-1, keepdims=True)
        expo = jnp.exp2(scores - top)
        total = jnp.sum(expo, axis=-1, keepdims=True)
        result = jnp.dot(expo.astype(BF16), load_v(low, high), preferred_element_type=F32)
        result = result * (1.0 / total)
        for part in range((high - low) // 128):
            piece = result[:, part * 128 : (part + 1) * 128]
            at = low // 128 + part
            if columns[at] is None:
                columns[at] = piece
            else:
                spot = lax.broadcasted_iota(jnp.int32, piece.shape, 1) + part * 128
                columns[at] = jnp.where(spot >= first, piece, columns[at])
    spot = lax.broadcasted_iota(jnp.int32, columns[-1].shape, 1)
    columns[-1] = jnp.where(spot < INNER - PADDED + 128, columns[-1], 0.0)
    return jnp.concatenate(columns, axis=1)


def kernel(
    frames, rows_axis,
    tiles_hbm, counts_hbm, x_hbm, sqkv_hbm, sout_hbm, tqkv_hbm, tout_hbm, out_hbm,
    key_tiles, tile_counts, xbuf, halo, w_s, w_t, o_s, o_t, qbuf, kbuf, vbuf,
    mixed, landed, heads, long_heads, rest, back, long_back, obuf,
    load_sem, x_sem, halo_send, halo_recv, go_send, go_recv,
    back_send, back_recv, long_send, long_recv, store_sem,
):
    frame = lax.axis_index("frame")
    row = lax.axis_index("row")
    above = lax.rem(row + rows_axis - 1, rows_axis)
    below = lax.rem(row + 1, rows_axis)
    feat = x_hbm.shape[-1]
    columns = x_hbm.shape[1]
    slab = TH * columns
    tile_rows = x_hbm.shape[0] // TH
    tile_cols = columns // TW
    tile_len = TH * TW
    group = slab // frames
    half_peers = frames // 2
    parity = lax.rem(frame, 2)
    my_block = parity * half_peers + frame // 2

    barrier = pltpu.get_barrier_semaphore()

    def greet(i, carry):
        pl.semaphore_signal(
            barrier, inc=1, device_id=(lax.rem(frame + i, frames), row), device_id_type=MESH
        )
        return carry

    lax.fori_loop(1, frames, greet, 0)
    for peer in (above, below):
        pl.semaphore_signal(barrier, inc=1, device_id=(frame, peer), device_id_type=MESH)

    def parts(src, dst):
        return [
            (src.at[pl.ds(n * INNER, INNER)], dst.at[pl.ds(n * PADDED, INNER)]) for n in (1, 2, 0)
        ]

    def load_rows(i):
        block = pl.ds(i * TH, TH)
        return pltpu.make_async_copy(x_hbm.at[block], xbuf.at[block], x_sem.at[i])

    pairs = parts(sqkv_hbm, w_s) + [(sout_hbm, o_s.at[pl.ds(0, INNER)])]
    pairs += [(tiles_hbm, key_tiles), (counts_hbm, tile_counts)]
    pairs += parts(tqkv_hbm, w_t) + [(tout_hbm, o_t.at[pl.ds(0, INNER)])]
    loads = [
        pltpu.make_async_copy(src, dst, load_sem.at[i]) for i, (src, dst) in enumerate(pairs)
    ]
    for i in range(tile_rows - 1):
        load_rows(i).start()
    for load in loads[:6]:
        load.start()
    load_rows(tile_rows - 1).start()
    for load in loads[6:]:
        load.start()
    pad_rows = jnp.zeros((PADDED - INNER, feat), BF16)
    for ref in (w_s, w_t):
        for n in range(3):
            ref[n * PADDED + INNER : (n + 1) * PADDED, :] = pad_rows
    o_s[INNER:, :] = pad_rows
    o_t[INNER:, :] = pad_rows

    def tiled(ref, first, low=0, high=tile_cols):
        return jnp.concatenate(
            [
                ref[pl.ds(first, TH), c * TW : (c + 1) * TW, :].reshape(tile_len, feat)
                for c in range(low, high)
            ],
            axis=0,
        )

    def project_queries(i):
        normed = layer_norm(tiled(xbuf, i * TH).astype(F32))
        result = lax.dot_general(normed, w_s[:PADDED, :], NT, preferred_element_type=F32)
        qbuf[i] = (result * SCALE).astype(BF16)

    def project_keys(ref, first, place):
        normed = layer_norm(tiled(ref, first).astype(F32))
        result = lax.dot_general(normed, w_s[PADDED:, :], NT, preferred_element_type=F32)
        kbuf[place] = result[:, :PADDED].astype(BF16)
        vbuf[place] = result[:, PADDED:].astype(BF16)

    def spatial(i, before_send):
        rows = tile_rows * row + i
        for half in range(2):
            marks = []
            for c in (2 * half, 2 * half + 1):
                tile = i * tile_cols + c
                count = tile_counts[0, tile]
                spot = lax.broadcasted_iota(jnp.int32, (tile_len, 9 * tile_len), 1) // tile_len
                mark = jnp.zeros((tile_len, 9 * tile_len), jnp.int32)
                for slot in range(key_tiles.shape[0]):
                    target = key_tiles[slot, 0, tile]
                    down = target // tile_cols - rows + 1
                    name = down * 3 + target % tile_cols - half
                    name = jnp.where(slot < count, name, -1)
                    mark = jnp.where(spot == name, 1, mark)
                marks.append(mark)
            keep = jnp.concatenate(marks, axis=0) > 0
            at = half * tile_len
            span = 2 * tile_len

            def load_q(low, high):
                return qbuf[i, 2 * at : 2 * at + span, low:high]

            def load_keys(ref):
                def load(low, high):
                    return jnp.concatenate(
                        [ref[i + d, at : at + 3 * tile_len, low:high] for d in range(3)], axis=0
                    )

                return load

            attended = attend(load_q, load_keys(kbuf), load_keys(vbuf), keep, NEG).astype(BF16)
            branch = jnp.dot(attended, o_s[...], preferred_element_type=F32)
            token = tiled(xbuf, i * TH, 2 * half, 2 * half + 2)
            result = token.astype(F32) + branch
            mixed[i, half * half_peers : (half + 1) * half_peers] = result.reshape(
                half_peers, group, feat
            ).astype(BF16)

            if half == 0:
                before_send()

            def send(k, carry):
                place = lax.rem(frame // 2 + k, half_peers)
                pltpu.make_async_remote_copy(
                    mixed.at[i, half * half_peers + place], landed.at[i, frame],
                    go_send.at[i], go_recv.at[i],
                    device_id=(2 * place + half, row), device_id_type=MESH,
                ).start()
                return carry

            own = parity if half else 1 - parity
            lax.fori_loop(own, half_peers, send, 0)
        landed[i, frame] = mixed[i, my_block]

    def send_back(src, dst, send_sem, recv_sem):
        def send(k, carry):
            peer = lax.rem(frame + k, frames)
            pltpu.make_async_remote_copy(
                src.at[peer], dst.at[my_block], send_sem, recv_sem,
                device_id=(peer, row), device_id_type=MESH,
            ).start()
            return carry

        dst[my_block] = src[frame]
        lax.fori_loop(1, frames, send, 0)

    def await_all(ref, sem):
        block = ref.at[pl.ds(0, frames - 1)]
        pltpu.make_async_copy(block, block, sem).wait()

    main = PADDED - 128
    left = INNER - main

    def temporal(i, pair, second):
        await_all(landed.at[i], go_recv.at[i])
        normed = layer_norm(landed[i].astype(F32).reshape(slab, feat))
        result = lax.dot_general(normed, w_t[...], NT, preferred_element_type=F32)
        queries = (result[:, :PADDED] * SCALE).astype(BF16)
        key_vecs = result[:, PADDED : 2 * PADDED].astype(BF16)
        val_vecs = result[:, 2 * PADDED :].astype(BF16)
        mine = lax.broadcasted_iota(jnp.int32, (slab, slab), 0) % group
        theirs = lax.broadcasted_iota(jnp.int32, (slab, slab), 1) % group
        attended = attend(
            lambda low, high: queries[:, low:high],
            lambda low, high: key_vecs[:, low:high],
            lambda low, high: val_vecs[:, low:high],
            mine == theirs,
            -jnp.inf,
        )
        if second:
            lane = lax.broadcasted_iota(jnp.int32, (slab, 128), 1)
            both = jnp.where(lane < left, rest[...], pltpu.roll(attended[:, main:], left, 1))
            whole = jnp.concatenate([attended[:, :main], both], axis=1)
            long_heads[pair] = whole.reshape(frames, group, PADDED).astype(BF16)
        else:
            heads[pair] = attended[:, :main].reshape(frames, group, main).astype(BF16)
            rest[...] = attended[:, main:]

    def send_first(pair):
        send_back(heads.at[pair], back.at[pair], back_send.at[pair], back_recv.at[pair])

    def send_second(pair):
        send_back(
            long_heads.at[pair], long_back.at[pair], long_send.at[pair], long_recv.at[pair]
        )

    def finish(i, pair, second):
        if second:
            long = long_back[pair].astype(F32).reshape(slab, PADDED)
            part = long[:, :main]
            tail = pltpu.roll(long[:, main:], left, 1)
        else:
            await_all(back.at[pair], back_recv.at[pair])
            await_all(long_back.at[pair], long_recv.at[pair])
            part = back[pair].astype(F32).reshape(slab, main)
            tail = long_back[pair, :, :, main:].astype(F32).reshape(slab, 128)
        attended = jnp.concatenate([part, tail], axis=1)
        branch = jnp.dot(attended.astype(BF16), o_t[...], preferred_element_type=F32)
        result = (mixed[i].astype(F32).reshape(slab, feat) + branch).astype(BF16)
        for c in range(tile_cols):
            obuf[pl.ds(i * TH, TH), c * TW : (c + 1) * TW, :] = result[
                c * tile_len : (c + 1) * tile_len
            ].reshape(TH, TW, feat)
        pltpu.make_async_copy(
            obuf.at[pl.ds(i * TH, TH)], out_hbm.at[pl.ds(i * TH, TH)], store_sem.at[i]
        ).start()

    last = tile_rows - 1

    def norm_first(i, carry):
        load_rows(i).wait()
        normed = layer_norm(tiled(xbuf, i * TH).astype(F32))
        obuf[pl.ds(i * TH, TH)] = normed.reshape(TH, columns, feat)
        return carry

    lax.fori_loop(0, last, norm_first, 0)
    for load in loads[:2]:
        load.wait()

    def first_keys(i, carry):
        normed = obuf[pl.ds(i * TH, TH)].reshape(slab, feat)
        result = lax.dot_general(normed, w_s[PADDED:, :], NT, preferred_element_type=F32)
        kbuf[i + 1] = result[:, :PADDED].astype(BF16)
        vbuf[i + 1] = result[:, PADDED:].astype(BF16)
        return carry

    lax.fori_loop(0, last, first_keys, 0)
    for load in loads[2:6]:
        load.wait()
    normed = obuf[TH : 2 * TH].reshape(slab, feat)
    result = lax.dot_general(normed, w_s[:PADDED, :], NT, preferred_element_type=F32)
    qbuf[1] = (result * SCALE).astype(BF16)

    send_down = pltpu.make_async_remote_copy(
        x_hbm.at[pl.ds(last * TH, TH)], halo.at[0], halo_send.at[0], halo_recv.at[0],
        device_id=(frame, below), device_id_type=MESH,
    )
    send_up = pltpu.make_async_remote_copy(
        x_hbm.at[pl.ds(0, TH)], halo.at[1], halo_send.at[1], halo_recv.at[1],
        device_id=(frame, above), device_id_type=MESH,
    )

    def meet():
        pl.semaphore_wait(barrier, frames + 1)
        send_down.start()
        send_up.start()

    spatial(1, meet)
    load_rows(last).wait()
    project_keys(xbuf, last * TH, tile_rows)

    def other_rows(n, carry):
        @pl.when(n == 1)
        def _():
            send_down.wait()
            send_up.wait()

            def halo_keys(k, carry):
                project_keys(halo.at[k], 0, k * (tile_rows + 1))
                return carry

            lax.fori_loop(0, 2, halo_keys, 0)

        i = jnp.where(n == 0, 2, (n - 1) * last)
        project_queries(i)
        spatial(i, lambda: None)
        return carry

    lax.fori_loop(0, last, other_rows, 0)

    for load in loads[6:]:
        load.wait()

    def place_of(pair, second):
        return (1 - pair) + second * (1 + (tile_rows - 2) * pair)

    def temporal_pair(pair, carry):
        temporal(place_of(pair, 0), pair, False)

        @pl.when(pair == 1)
        def _():
            for i in range(tile_rows):
                await_all(landed.at[i], go_send.at[i])
            send_first(0)
            send_second(0)
            send_first(1)

        temporal(place_of(pair, 1), pair, True)
        return carry

    lax.fori_loop(0, 2, temporal_pair, 0)
    send_second(1)

    def finish_pair(pair, carry):
        for second in range(2):
            finish(place_of(pair, second), pair, bool(second))
        return carry

    lax.fori_loop(0, 2, finish_pair, 0)

    for pair in range(2):
        await_all(back.at[pair], back_send.at[pair])
        await_all(long_back.at[pair], long_send.at[pair])
    for i in range(tile_rows):
        pltpu.make_async_copy(
            obuf.at[pl.ds(i * TH, TH)], out_hbm.at[pl.ds(i * TH, TH)], store_sem.at[i]
        ).wait()


def body(frames_in, spatial_qkv, spatial_out, temporal_qkv, temporal_out, key_tiles, tile_counts):
    frames = lax.axis_size("frame")
    rows_axis = lax.axis_size("row")
    rows, columns, feat = frames_in.shape[1:]
    slab = TH * columns
    tile_rows = rows // TH
    group = slab // frames
    dma = pltpu.SemaphoreType.DMA
    hbm = pl.BlockSpec(memory_space=pltpu.HBM)
    result = pl.pallas_call(
        functools.partial(kernel, frames, rows_axis),
        out_shape=jax.ShapeDtypeStruct((rows, columns, feat), BF16),
        in_specs=[hbm] * 7,
        out_specs=pl.BlockSpec(memory_space=pl.ANY),
        scratch_shapes=[
            pltpu.SMEM(key_tiles.shape[2:] + (1, key_tiles.shape[1]), jnp.int32),
            pltpu.SMEM(tile_counts.shape, jnp.int32),
            pltpu.VMEM((rows, columns, feat), BF16),
            pltpu.VMEM((2, TH, columns, feat), BF16),
            pltpu.VMEM((3 * PADDED, feat), BF16),
            pltpu.VMEM((3 * PADDED, feat), BF16),
            pltpu.VMEM((PADDED, feat), BF16),
            pltpu.VMEM((PADDED, feat), BF16),
            pltpu.VMEM((tile_rows, slab, PADDED), BF16),
            pltpu.VMEM((tile_rows + 2, slab, PADDED), BF16),
            pltpu.VMEM((tile_rows + 2, slab, PADDED), BF16),
            pltpu.VMEM((tile_rows, frames, group, feat), BF16),
            pltpu.VMEM((tile_rows, frames, group, feat), BF16),
            pltpu.VMEM((2, frames, group, PADDED - 128), BF16),
            pltpu.VMEM((2, frames, group, PADDED), BF16),
            pltpu.VMEM((slab, 128), F32),
            pltpu.VMEM((2, frames, group, PADDED - 128), BF16),
            pltpu.VMEM((2, frames, group, PADDED), BF16),
            pltpu.VMEM((rows, columns, feat), BF16),
            dma((10,)),
            dma((tile_rows,)),
            dma((2,)),
            dma((2,)),
            dma((tile_rows,)),
            dma((tile_rows,)),
            dma((2,)),
            dma((2,)),
            dma((2,)),
            dma((2,)),
            dma((tile_rows,)),
        ],
        compiler_params=pltpu.CompilerParams(
            collective_id=0, has_side_effects=True, vmem_limit_bytes=44 * 2**20
        ),
    )(
        *(
            pltpu.with_memory_space_constraint(array, pltpu.HBM)
            for array in (
                jnp.transpose(key_tiles, (2, 0, 1)), tile_counts, frames_in[0],
                spatial_qkv.T, spatial_out, temporal_qkv.T, temporal_out,
            )
        )
    )
    return result[None]


def solution(mesh):
    in_specs = (
        P("frame", "row", None, None),
        P(),
        P(),
        P(),
        P(),
        P("frame", "row", None),
        P("frame", "row"),
    )
    out_specs = P("frame", "row", None, None)
    return jax.shard_map(body, mesh=mesh, in_specs=in_specs, out_specs=out_specs, check_vma=False)
```
